256 devices in a mesh: expert: 32 (over z, y), replica: 8 (over x, core).
Axes of the slice: x: 4, y: 4, z: 8, core: 2. Of those that a mesh axis runs over, the one named last changes fastest.
Arguments:
- tokens: bfloat16 [16384, 2880], P(('expert', 'replica')), may hold values from -6 to 6
- expert_ids: int32 [16384, 4], P(('expert', 'replica')), may hold values from 0 to 31, all different within a row; in each aligned block of 64 rows (0 to 63, 64 to 127, ...) at most 12 rows name the same one
- gate_codes: int32 [16384, 4], P(('expert', 'replica')), may hold values from 1 to 65535
- w_gate: bfloat16 [32, 2880, 2880], P('expert', None, 'replica'), may hold values from -0.109375 to 0.109375
- w_up: bfloat16 [32, 2880, 2880], P('expert', None, 'replica'), may hold values from -0.109375 to 0.109375
- w_down: bfloat16 [32, 2880, 2880], P('expert', 'replica'), may hold values from -0.109375 to 0.109375
Outputs:
- mixed: bfloat16 [16384, 2880], P(('expert', 'replica'))
The draws below stay inside these ranges and needn't reach their ends.
Inputs may be any that keep to these rules, and one draw needn't show every extreme that they name: `expert_ids`: each row names 4 different experts. Among the 64 rows of one device each expert is named at most 12 times, a bound that some block reaches.
All inputs are finite; a program needn't handle non-finite values.
Results may differ from the reference program's by a relative error of at most 0.015.
Values may be sent and summed in bfloat16 or wider, within the bound.
No kernel may reach another device: no remote copies, remote signals or barrier semaphores. Data moves between devices by JAX's collectives and lax.ppermute only.
A program may use at most 128 MiB of HBM per device.

```python
import math
import jax
import jax.numpy as jnp
import numpy as np
from jax import lax

D = 2880
FF = 2880
TOP = 4
TOK_DEV = 64
EXPERTS = 32
CAP = 12
TOKENS = 16384
N_EXPERT = 32
N_REPLICA = 8


def with_ends(entries, stream_key, smallest, largest):
    index_at = [jax.random.randint(jax.random.fold_in(stream_key, axis), (), 0, length) for axis, length in enumerate(entries.shape)]
    longest = entries.shape.index(max(entries.shape))
    next_to = index_at[:longest] + [(index_at[longest] + 1) % entries.shape[longest]] + index_at[longest + 1:]
    return entries.at[tuple(index_at)].set(smallest).at[tuple(next_to)].set(largest)


def block_levels(key, extent, shards, low, top_value):
    level, own = 1.0, jax.random.fold_in(key, 6)
    for position, blocks in shards:
        draws = jnp.exp(jax.random.uniform(jax.random.fold_in(own, position), (blocks,), jnp.float32, low / len(shards), top_value / len(shards)))
        level = level * jnp.repeat(draws, extent[position] // blocks).reshape([-1 if axis == position else 1 for axis in range(len(extent))])
    return level


def deal_out(stream_key, own, number, rows, number_of, top, reach, lean):
    order = jax.random.permutation(stream_key, number_of)
    crowded, usual = shares(number_of, rows * top, reach, lean, True), shares(number_of, rows * top, reach, lean, False)
    places = jnp.arange(number_of)

    def named(sizes, turn):
        used = int((sizes > 0).sum())
        fixed = max(1, used // 4)
        passed = fixed + (places - fixed + turn * (used - fixed)) % max(1, number_of - fixed)
        return jnp.zeros((number_of,), jnp.int32).at[order[jnp.where(places < fixed, places, passed)]].set(jnp.asarray(sizes, jnp.int32))

    sizes = jnp.where(number % 4 == 0, named(crowded, number // 4), named(usual, number - number // 4 - 1))
    mixed = jax.random.permutation(jax.random.fold_in(own, 3), number_of)
    donor, receiver = mixed[0:number_of // 2 * 2:2], mixed[1:number_of // 2 * 2:2]
    margin = jnp.minimum(sizes[donor] - 1, reach - sizes[receiver]) // 2
    margin = jnp.where((donor == order[0]) | (receiver == order[0]) | (sizes[receiver] == 0), 0, jnp.maximum(margin, 0))
    passed = jax.random.randint(jax.random.fold_in(own, 4), (number_of // 2,), 0, 1 << 20) % (margin + 1)
    sizes = sizes.at[donor].add(-passed).at[receiver].add(passed)
    items = jnp.searchsorted(jnp.cumsum(sizes), jnp.arange(rows * top), side="right").astype(jnp.int32)
    listing = items.reshape(top, rows).T
    listing = listing[jax.random.permutation(jax.random.fold_in(own, 1), rows)]
    turn = jax.random.randint(jax.random.fold_in(own, 2), (rows, 1), 0, top)
    return jnp.take_along_axis(listing, (jnp.arange(top)[None, :] + turn) % top, axis=1)


def shares(amount, total, reach, slope, full):
    loads = [(1 << 20) // math.isqrt(standing ** slope) + 1 for standing in range(1, amount + 1)]
    largest = reach if full else min(reach, max(-(-total // amount), total * loads[0] // sum(loads)))
    least = 1 if total - largest >= amount - 1 else 0
    given, spare = [largest] + [least] * (amount - 1), total - largest - least * (amount - 1)
    while spare > 0:
        free = [i for i in range(1, amount) if given[i] < largest] or [i for i in range(1, amount) if given[i] < reach]
        whole, remaining = sum([loads[i] for i in free]), spare
        for i in free:
            addition = min(reach - given[i], max(1, remaining * loads[i] // whole), spare)
            given[i] = given[i] + addition
            spare = spare - addition
    return np.array(given)


def centred(stream_key, extent, width, reach, pieces=(), held_as=jnp.bfloat16):
    array = width * jax.random.normal(stream_key, extent, jnp.float32)
    if pieces:
        array = array * block_levels(stream_key, extent, pieces, -0.22, 0.18)
    return jnp.clip(array, -reach, reach).astype(held_as)


def setup_inputs(seed: int = 0) -> dict:
    arg_keys = jax.random.split(jax.random.key(seed), 7)
    tokens = centred(arg_keys[0], (TOKENS, D), 1.0, 6.0, ((0, 256),))
    expert_ids_keys = jax.random.split(jax.random.fold_in(arg_keys[1], 1), TOKENS // TOK_DEV)
    expert_ids_turns = jax.random.permutation(jax.random.fold_in(arg_keys[1], 3), TOKENS // TOK_DEV)
    expert_ids = jax.vmap(lambda own, number: deal_out(jax.random.fold_in(arg_keys[1], 2), own, number, TOK_DEV, EXPERTS, TOP, CAP, 2))(expert_ids_keys, expert_ids_turns).reshape((TOKENS, TOP))
    gate_codes = with_ends(jax.random.randint(arg_keys[2], (TOKENS, TOP), 1, 65536), jax.random.fold_in(arg_keys[2], 1), 1, 65535).astype(jnp.int32)
    w_gate = centred(arg_keys[3], (EXPERTS, D, FF), D ** -0.5, 0.109375, ((0, 32), (2, 8)))
    w_up = centred(arg_keys[4], (EXPERTS, D, FF), D ** -0.5, 0.109375, ((0, 32), (2, 8)))
    w_down = centred(arg_keys[5], (EXPERTS, FF, D), FF ** -0.5, 0.109375, ((0, 32), (1, 8)))
    return {"tokens": tokens, "expert_ids": expert_ids, "gate_codes": gate_codes, "w_gate": w_gate, "w_up": w_up, "w_down": w_down}


def activate(gate, up):
    return gate * jax.nn.sigmoid(1.702 * gate) * (up + 1.0)


def reference(tokens, expert_ids, gate_codes, w_gate, w_up, w_down):
    count_rows = tokens.shape[0]
    flat_ids = expert_ids.reshape(-1)
    gates = gate_codes.reshape(-1).astype(jnp.float32) / 65536.0
    most_rows = N_EXPERT * N_REPLICA * CAP
    part_width = FF // N_REPLICA

    def one_expert(expert, total):
        chosen = flat_ids == expert
        count = jnp.sum(chosen.astype(jnp.int32))
        where = jnp.nonzero(chosen, size=most_rows, fill_value=0)[0].astype(jnp.int32)
        valid = (jnp.arange(most_rows, dtype=jnp.int32) < count).astype(jnp.float32)
        owner = (where // TOP).astype(jnp.int32)
        rows = tokens[owner]
        gate = jnp.dot(rows, w_gate[expert], preferred_element_type=jnp.float32)
        up = jnp.dot(rows, w_up[expert], preferred_element_type=jnp.float32)
        hidden = activate(gate, up).astype(jnp.bfloat16)
        result = jnp.zeros((most_rows, D), jnp.float32)
        for part in range(N_REPLICA):
            piece = jnp.dot(hidden[:, part * part_width:(part + 1) * part_width],
                            w_down[expert, part * part_width:(part + 1) * part_width],
                            preferred_element_type=jnp.float32).astype(jnp.bfloat16)
            piece = lax.optimization_barrier(piece)
            result = result + piece.astype(jnp.float32)
        rounded = lax.optimization_barrier(result.astype(jnp.bfloat16))
        weight = gates[where] * valid
        return total.at[owner].add(rounded.astype(jnp.float32) * weight[:, None])

    total = lax.fori_loop(0, EXPERTS, one_expert, jnp.zeros((count_rows, D), jnp.float32))
    return total.astype(jnp.bfloat16)
```

```python
import functools

import jax
import jax.numpy as jnp
from jax import lax
from jax.experimental import pallas as pl
from jax.experimental.pallas import tpu as pltpu
from jax.sharding import Mesh, PartitionSpec as P

F32 = jnp.float32
BF16 = jnp.bfloat16
NZ, NY, NX, NC = 8, 4, 4, 2
TOK = 64
WIDTH = 2880
PART = 360
CHUNKS = ((0, 4), (4, 4), (8, 4))
ALL_TOK = NY * TOK


def params(limit=60):
    return pltpu.CompilerParams(vmem_limit_bytes=limit * 1024 * 1024)


def slots(rank, first, count):
    rows = 4 * count
    wide = jnp.broadcast_to(rank[:, None, :], (NZ, rows, ALL_TOK)).reshape(NZ * rows, ALL_TOK)
    row = lax.broadcasted_iota(jnp.int32, (NZ * rows, ALL_TOK), 0)
    column = lax.broadcasted_iota(jnp.int32, (NZ * rows, ALL_TOK), 1)
    within = lax.rem(row, rows)
    slot = first + lax.rem(within, count)
    return (wide == slot.astype(F32)) & (lax.div(within, count) == lax.div(column, TOK))


def select_kernel(chunks, meta_ref, y_ref, tokens_ref, *out_refs):
    expert = lax.broadcasted_iota(jnp.int32, (NZ, ALL_TOK), 0) * NY + y_ref[0]
    named = jnp.zeros((NZ, ALL_TOK), F32)
    gate = jnp.zeros((NZ, ALL_TOK), F32)
    for k in range(4):
        hit = meta_ref[k : k + 1, :] == expert
        named = named + jnp.where(hit, 1.0, 0.0)
        gate = gate + jnp.where(hit, meta_ref[4 + k : 5 + k, :].astype(F32) / 65536.0, 0.0)
    row = lax.broadcasted_iota(jnp.int32, (ALL_TOK, ALL_TOK), 0)
    column = lax.broadcasted_iota(jnp.int32, (ALL_TOK, ALL_TOK), 1)
    earlier = jnp.where((row < column) & (lax.div(row, TOK) == lax.div(column, TOK)), 1.0, 0.0)
    rank = jnp.dot(named.astype(BF16), earlier.astype(BF16), preferred_element_type=F32)
    rank = jnp.where(named > 0.5, rank, -1.0)
    out_refs[0][...] = rank
    out_refs[1][...] = gate
    for out_ref, (first, count) in zip(out_refs[2:], chunks):
        picker = jnp.where(slots(rank, first, count), 1.0, 0.0).astype(BF16)
        out_ref[...] = jnp.dot(picker, tokens_ref[...], preferred_element_type=F32).astype(BF16)


def select(meta, y_index, tokens):
    whole = pl.BlockSpec(memory_space=pltpu.VMEM)
    return pl.pallas_call(
        functools.partial(select_kernel, CHUNKS),
        in_specs=[whole, pl.BlockSpec(memory_space=pltpu.SMEM), whole],
        out_specs=[whole] * (2 + len(CHUNKS)),
        out_shape=[jax.ShapeDtypeStruct((NZ, ALL_TOK), F32)] * 2
        + [jax.ShapeDtypeStruct((NZ * NY * count, WIDTH), BF16) for _, count in CHUNKS],
        compiler_params=params(),
        name="select_rows",
    )(meta, y_index, tokens)


def ffn_kernel(n_rows, *refs):
    row_refs = refs[:n_rows]
    weight_refs = refs[n_rows : n_rows + 6]
    out_refs = refs[n_rows + 6 : 2 * n_rows + 6]
    x_ref, y_ref, wg_ref, wu_ref, wd_ref, in_sems, weight_sems, out_sems = refs[2 * n_rows + 6 :]
    held = (wg_ref, wu_ref, wd_ref)
    loads = [
        pltpu.make_async_copy(ref, held[i % 3].at[i // 3], weight_sems.at[i])
        for i, ref in enumerate(weight_refs)
    ]
    starts = []
    at = 0
    for ref in row_refs:
        starts.append(at)
        at += ref.shape[0]
    rows = [
        pltpu.make_async_copy(ref, x_ref.at[pl.ds(first, ref.shape[0])], in_sems.at[i])
        for i, (ref, first) in enumerate(zip(row_refs, starts))
    ]
    for load in rows[:1] + loads + rows[1:]:
        load.start()
    for load in rows + loads:
        load.wait()
    across = (((1,), (1,)), ((), ()))
    groups, high, width = x_ref.shape
    step = groups // 2
    tall = step * high

    def body(i, carry):
        x = x_ref[pl.ds(i * step, step)].reshape(tall, width)

        def half(w, total):
            gate = lax.dot_general(x, wg_ref[w], across, preferred_element_type=F32)
            up = lax.dot_general(x, wu_ref[w], across, preferred_element_type=F32)
            hidden = (gate * jax.nn.sigmoid(1.702 * gate) * (up + 1.0)).astype(BF16)
            return total + jnp.dot(hidden, wd_ref[w], preferred_element_type=F32)

        total = lax.fori_loop(0, 2, half, jnp.zeros((tall, width), F32))
        y_ref[pl.ds(i * step, step)] = total.astype(BF16).reshape(step, high, width)
        return carry

    lax.fori_loop(0, 2, body, 0)
    stores = [
        pltpu.make_async_copy(y_ref.at[pl.ds(first, ref.shape[0])], ref, out_sems.at[i])
        for i, (ref, first) in enumerate(zip(out_refs, starts))
    ]
    for store in stores:
        store.start()
    for store in stores:
        store.wait()


def ffn(rows, weights):
    anywhere = pl.BlockSpec(memory_space=pl.ANY)
    count = sum(r.shape[0] for r in rows)
    high = rows[0].shape[1]
    flops = count * high * WIDTH * PART * 2 * 6
    moved = count * high * WIDTH * 4 + 12 * WIDTH * PART
    return pl.pallas_call(
        functools.partial(ffn_kernel, len(rows)),
        in_specs=[anywhere] * (len(rows) + 6),
        out_specs=[anywhere] * len(rows),
        out_shape=[jax.ShapeDtypeStruct(r.shape, BF16) for r in rows],
        scratch_shapes=[
            pltpu.VMEM((count, high, WIDTH), BF16),
            pltpu.VMEM((count, high, WIDTH), BF16),
            pltpu.VMEM((2, PART, WIDTH), BF16),
            pltpu.VMEM((2, PART, WIDTH), BF16),
            pltpu.VMEM((2, PART, WIDTH), BF16),
            pltpu.SemaphoreType.DMA((len(rows),)),
            pltpu.SemaphoreType.DMA((6,)),
            pltpu.SemaphoreType.DMA((len(rows),)),
        ],
        compiler_params=params(),
        cost_estimate=pl.CostEstimate(flops=flops, transcendentals=0, bytes_accessed=moved),
        name="ffn",
    )(*rows, *weights)


def combine_kernel(first, count, rank_ref, gate_ref, back_ref, *refs):
    rows = 4 * count
    chosen = slots(rank_ref[...], first, count)
    wide = jnp.broadcast_to(gate_ref[...][:, None, :], (NZ, rows, ALL_TOK)).reshape(NZ * rows, ALL_TOK)
    weight = jnp.where(chosen, wide, 0.0)
    high = weight.astype(BF16)
    low = (weight - high.astype(F32)).astype(BF16)
    along = (((0,), (0,)), ((), ()))
    back = back_ref[...]
    total = lax.dot_general(high, back, along, preferred_element_type=F32)
    total = total + lax.dot_general(low, back, along, preferred_element_type=F32)
    if len(refs) == 2:
        total = total + refs[0][...]
    refs[-1][...] = total.astype(refs[-1].dtype)


def combine(first, count, rank, gate, back, before, dtype):
    whole = pl.BlockSpec(memory_space=pltpu.VMEM)
    operands = (rank, gate, back) + (() if before is None else (before,))
    return pl.pallas_call(
        functools.partial(combine_kernel, first, count),
        in_specs=[whole] * len(operands),
        out_specs=whole,
        out_shape=jax.ShapeDtypeStruct((ALL_TOK, WIDTH), dtype),
        compiler_params=params(),
        name="combine",
    )(*operands)


def add(*parts):
    total = parts[0].astype(F32)
    for part in parts[1:]:
        total = total + part.astype(F32)
    return total.astype(BF16)


RIGHT = [(i, (i + 1) % NX) for i in range(NX)]
LEFT = [(i, (i - 1) % NX) for i in range(NX)]


def on_device(tokens, expert_ids, gate_codes, w_gate, w_up, w_down):
    mine = (jnp.swapaxes(w_gate[0], 0, 1), jnp.swapaxes(w_up[0], 0, 1), w_down[0])
    other = tuple(lax.ppermute(w, "c", [(0, 1), (1, 0)]) for w in mine)
    weights = mine + other
    meta = jnp.concatenate([expert_ids.T, gate_codes.T], axis=0)
    meta = lax.all_to_all(jnp.broadcast_to(meta[None], (NY, 8, TOK)), "y", 0, 0, tiled=True)
    meta = meta.transpose(1, 0, 2).reshape(8, ALL_TOK)
    near = lax.all_to_all(jnp.broadcast_to(tokens[None], (NY, TOK, WIDTH)), "y", 0, 0, tiled=True)
    near = near.reshape(ALL_TOK, WIDTH)
    y_index = lax.axis_index("y").astype(jnp.int32).reshape(1)
    rank, gate, *outgoing = select(meta, y_index, near)
    total = None
    for index, (first, count) in enumerate(CHUNKS):
        rows = NZ * NY * count
        half = NZ // 2
        block = lax.all_to_all(outgoing[index].reshape(NZ, NY * count, WIDTH), "z", 0, 0, tiled=True)
        left = lax.ppermute(block, "x", RIGHT)
        right = lax.ppermute(block, "x", LEFT)
        far_a = lax.ppermute(left[:half], "x", RIGHT)
        far_b = lax.ppermute(right[half:], "x", LEFT)
        own, to_left, to_right, to_far_a, to_far_b = ffn((block, left, right, far_a, far_b), weights)
        pass_right = lax.ppermute(to_far_a, "x", RIGHT)
        pass_left = lax.ppermute(to_far_b, "x", LEFT)
        to_right = jnp.concatenate([add(to_right[:half], pass_right), to_right[half:]], axis=0)
        to_left = jnp.concatenate([to_left[:half], add(to_left[half:], pass_left)], axis=0)
        from_left = lax.ppermute(to_right, "x", RIGHT)
        from_right = lax.ppermute(to_left, "x", LEFT)
        summed = add(own, from_left, from_right)
        back = lax.all_to_all(summed, "z", 0, 0, tiled=True)
        last = index == len(CHUNKS) - 1
        total = combine(first, count, rank, gate, back.reshape(rows, WIDTH), total, BF16 if last else F32)
    parts = lax.all_to_all(total.reshape(NY, TOK, WIDTH), "y", 0, 0, tiled=True)
    return jnp.sum(parts.astype(F32), axis=0).astype(BF16)


def solution(mesh):
    fine = Mesh(mesh.devices.reshape(NZ, NY, NX, NC), ("z", "y", "x", "c"))
    return jax.shard_map(
        on_device,
        mesh=fine,
        in_specs=(
            P(("z", "y", "x", "c"), None),
            P(("z", "y", "x", "c"), None),
            P(("z", "y", "x", "c"), None),
            P(("z", "y"), None, ("x", "c")),
            P(("z", "y"), None, ("x", "c")),
            P(("z", "y"), ("x", "c"), None),
        ),
        out_specs=P(("z", "y", "x", "c"), None),
        check_vma=False,
    )
```
